32 devices in a mesh: ctx: 8 (over z, y), head: 4 (over x, core).
Axes of the slice: x: 2, y: 2, z: 4, core: 2. Of those that a mesh axis runs over, the one named last changes fastest.
Arguments:
- queries: bfloat16 [2048, 6144], P(('ctx', 'head')), may hold values from -42 to 42
- key_head_columns: bfloat16 [2048, 512], P(('ctx', 'head')), may hold values from -4 to 4
- value_head_columns: bfloat16 [2048, 512], P(('ctx', 'head')), may hold values from -6 to 6
- output_gradient: bfloat16 [2048, 6144], P(('ctx', 'head')), may hold values from -6 to 6
- file_starts: int32 [5], replicated, may hold values from 0 to 1984, as said below
- file_imports: int32 [5, 4], replicated, may hold values from -1 to 4, as said below
- header_lens: int32 [5], replicated, may hold values from 16 to 64
Outputs:
- grad_queries: float32 [2048, 6144], P(('ctx', 'head'))
- key_gradient: float32 [2048, 512], P(('ctx', 'head'))
- value_gradient: float32 [2048, 512], P(('ctx', 'head'))
The draws below stay inside these ranges and needn't reach their ends.
Inputs may be any that keep to these rules, and one draw needn't show every extreme that they name: `file_starts`: Increasing; the first is 0 and the last is 1984; each is a multiple of 64; no two lie in the same aligned block of 256 tokens; each file has 64 tokens or more. `file_imports`: each row lists distinct files other than its own, then -1 in the unused places; file 0 imports nothing.
All inputs are finite; a program needn't handle non-finite values.
Results may differ from the reference program's by a relative error of at most 0.004.
Values may be sent and summed in bfloat16 or wider, within the bound.
No kernel may reach another device: no remote copies, remote signals or barrier semaphores. Data moves between devices by JAX's collectives and lax.ppermute only.
A program may use at most 64 MiB of HBM per device.

```python
import math
import jax
import jax.numpy as jnp
from jax import lax

QUERY_HEADS = 48
KEY_VALUE_HEADS = 4
HEAD_WIDTH = 128
TOK_DEV = 256
WIN = 1024
HDR = 64
IMPORTS = 4
PACKED_TOKENS = 2048
FILES = 5


def shared_pair(key):
    base = jax.random.fold_in(key, 11)
    leading_key = jax.random.fold_in(base, 1)
    second_key = jax.random.fold_in(base, 2)
    unpadded_keys = jnp.clip(jax.random.normal(leading_key, (PACKED_TOKENS, KEY_VALUE_HEADS * HEAD_WIDTH), jnp.float32), -4.0, 4.0)
    query_raw = jnp.clip(jax.random.normal(second_key, (PACKED_TOKENS, QUERY_HEADS * HEAD_WIDTH), jnp.float32), -4.0, 4.0)
    return (query_raw, unpadded_keys)


def draw_queries(key, part):
    return shared_pair(key)[0].astype(jnp.bfloat16)


def draw_key_head_columns(key, part):
    return shared_pair(key)[1].astype(jnp.bfloat16)


def draw_file_starts(key, part):
    base = jax.random.fold_in(key, 21)
    shards = PACKED_TOKENS // TOK_DEV
    order = jax.random.permutation(jax.random.fold_in(base, 1), shards - 2) + 1
    chosen = jnp.sort(order[:FILES - 2])
    within = jax.random.randint(jax.random.fold_in(base, 2), (FILES - 2,), 0, TOK_DEV // HDR) * HDR
    middle = (chosen * TOK_DEV + within).astype(jnp.int32)
    last_start = jnp.full((1,), PACKED_TOKENS - HDR, jnp.int32)
    return jnp.concatenate([jnp.zeros((1,), jnp.int32), middle, last_start]).astype(jnp.int32)


def draw_file_imports(key, part):
    base = jax.random.fold_in(key, 31)
    files = jnp.arange(FILES, dtype=jnp.int32)
    favour = jax.random.randint(jax.random.fold_in(base, 1), (FILES,), 0, 8)
    noise = jax.random.randint(jax.random.fold_in(base, 2), (FILES, FILES), 0, 32)
    scores = (noise + favour[None, :] * favour[None, :]) * FILES + files[None, :]
    scores = jnp.where(files[:, None] == files[None, :], -1, scores)
    scores = jnp.where((files[:, None] == FILES - 2) & (files[None, :] == FILES - 1), 1000 * FILES, scores)
    picked = lax.top_k(scores, IMPORTS)[1].astype(jnp.int32)
    counts = jax.random.randint(jax.random.fold_in(base, 3), (FILES,), 0, IMPORTS + 1)
    counts = jnp.where(files == 0, 0, counts)
    counts = jnp.where(files == FILES - 2, jnp.maximum(counts, 1), counts)
    counts = jnp.where(files == FILES - 1, IMPORTS, counts)
    places = jnp.arange(IMPORTS, dtype=jnp.int32)
    return jnp.where(places[None, :] < counts[:, None], picked, -1).astype(jnp.int32)


def place_ends(result, rng, smallest, high):
    index_at = [jax.random.randint(jax.random.fold_in(rng, axis), (), 0, length) for axis, length in enumerate(result.shape)]
    main_axis = result.shape.index(max(result.shape))
    neighbour = index_at[:main_axis] + [(index_at[main_axis] + 1) % result.shape[main_axis]] + index_at[main_axis + 1:]
    return result.at[tuple(index_at)].set(smallest).at[tuple(neighbour)].set(high)


def block_scale(rng, shape, cuts, smallest, high):
    factor_of = 1.0
    for axis_at, blocks in cuts:
        draws = jax.random.uniform(jax.random.fold_in(jax.random.fold_in(rng, 6), axis_at), (blocks,), jnp.float32, smallest / len(cuts), high / len(cuts))
        factor_of = factor_of * jnp.repeat(jnp.exp(draws), shape[axis_at] // blocks).reshape((-1,) + (1,) * (len(shape) - 1 - axis_at))
    return factor_of


def gaussian(key, extent, width, most, cuts=(), kind=jnp.bfloat16):
    gain = block_scale(key, extent, cuts, -0.22, 0.18) if cuts else 1.0
    values = jax.random.normal(key, extent, jnp.float32) * width * gain
    return jnp.minimum(jnp.maximum(values, -most), most).astype(kind)


def setup_inputs(seed: int = 0) -> dict:
    seeds = jax.random.split(jax.random.key(seed), 8)
    queries = draw_queries(jax.random.fold_in(seeds[7], 71), 0)
    key_head_columns = draw_key_head_columns(jax.random.fold_in(seeds[7], 71), 0)
    value_head_columns = gaussian(seeds[2], (PACKED_TOKENS, KEY_VALUE_HEADS * HEAD_WIDTH), 1.0, 6.0, ((0, 32),))
    output_gradient = gaussian(seeds[3], (PACKED_TOKENS, QUERY_HEADS * HEAD_WIDTH), 1.0, 6.0, ((0, 32),))
    file_starts = draw_file_starts(jax.random.fold_in(seeds[7], 71), 0)
    file_imports = draw_file_imports(jax.random.fold_in(seeds[7], 71), 0)
    header_lens = place_ends(jax.random.randint(seeds[6], (FILES,), HDR // 4, HDR + 1), jax.random.fold_in(seeds[6], 1), HDR // 4, HDR).astype(jnp.int32)
    return dict(queries=queries, key_head_columns=key_head_columns, value_head_columns=value_head_columns, output_gradient=output_gradient, file_starts=file_starts, file_imports=file_imports, header_lens=header_lens)


def local_files(file_starts, file_imports, header_lens, offset_base, span_rows):
    places = offset_base + jnp.arange(span_rows, dtype=jnp.int32)
    before = file_starts[None, :] <= places[:, None]
    file_of = lax.optimization_barrier(jnp.sum(before.astype(jnp.int32), axis=1)).astype(jnp.int32) - 1
    file_begin = lax.optimization_barrier(jnp.max(jnp.where(before, file_starts[None, :], 0), axis=1)).astype(jnp.int32)
    lower_file = file_of[0]
    upper_file = file_of[span_rows - 1]
    per_file = file_imports.shape[1]
    lower_list = lax.dynamic_slice_in_dim(file_imports, lower_file.astype(jnp.int32), 1, 0)[0]
    upper_list = lax.dynamic_slice_in_dim(file_imports, upper_file.astype(jnp.int32), 1, 0)[0]
    targets = jnp.concatenate([lower_list, upper_list])
    source_file = jnp.concatenate([jnp.full((per_file,), lower_file, jnp.int32), jnp.full((per_file,), upper_file, jnp.int32)])
    usable = (targets >= 0) & ((jnp.arange(2 * per_file, dtype=jnp.int32) < per_file) | (upper_file != lower_file))
    matches = jnp.arange(file_starts.shape[0], dtype=jnp.int32)[None, :] == targets[:, None]
    target_start = lax.optimization_barrier(jnp.sum(jnp.where(matches, file_starts[None, :], 0), axis=1)).astype(jnp.int32)
    target_len = lax.optimization_barrier(jnp.sum(jnp.where(matches, header_lens[None, :], 0), axis=1)).astype(jnp.int32)
    return (places, file_of, file_begin, source_file, usable, target_start, target_len)

def visibility(places, file_of, file_begin, key_places, source_file, usable, target_len):
    window_ok = (key_places[None, :] <= places[:, None]) & (key_places[None, :] > places[:, None] - WIN) & (key_places[None, :] >= file_begin[:, None])
    offsets = jnp.arange(usable.shape[0] * HDR, dtype=jnp.int32) % HDR
    header_ok = jnp.repeat(usable, HDR) & (offsets < jnp.repeat(target_len, HDR))
    header_vis = header_ok[None, :] & (file_of[:, None] == jnp.repeat(source_file, HDR)[None, :])
    return jnp.concatenate([window_ok, header_vis], axis=1)

def reference(queries, key_head_columns, value_head_columns, output_gradient, file_starts, file_imports, header_lens):
    queries_per_group = QUERY_HEADS // KEY_VALUE_HEADS
    scaling = 1.0 / math.sqrt(HEAD_WIDTH)
    reach = WIN // TOK_DEV
    shards = PACKED_TOKENS // TOK_DEV
    front_padding = reach * TOK_DEV
    keys_rank_three = key_head_columns.reshape(PACKED_TOKENS, KEY_VALUE_HEADS, HEAD_WIDTH)
    values_rank_three = value_head_columns.reshape(PACKED_TOKENS, KEY_VALUE_HEADS, HEAD_WIDTH)
    padded_keys = jnp.concatenate([jnp.zeros((front_padding, KEY_VALUE_HEADS, HEAD_WIDTH), key_head_columns.dtype), keys_rank_three], axis=0)
    padded_values = jnp.concatenate([jnp.zeros((front_padding, KEY_VALUE_HEADS, HEAD_WIDTH), value_head_columns.dtype), values_rank_three], axis=0)
    query_rank_four = queries.reshape(PACKED_TOKENS, KEY_VALUE_HEADS, queries_per_group, HEAD_WIDTH)
    gradient_rank_four = output_gradient.reshape(PACKED_TOKENS, KEY_VALUE_HEADS, queries_per_group, HEAD_WIDTH)
    block_count = 2 * IMPORTS

    def one_shard(carry, shard_index):
        key_gradient_sum, value_gradient_sum = carry
        offset_base = (shard_index * TOK_DEV).astype(jnp.int32)
        places, file_of, file_begin, source_file, usable, target_start, target_len = local_files(file_starts, file_imports, header_lens, offset_base, TOK_DEV)
        key_places = offset_base - front_padding + jnp.arange(front_padding + TOK_DEV, dtype=jnp.int32)
        key_window = lax.dynamic_slice_in_dim(padded_keys, offset_base, front_padding + TOK_DEV, 0)
        value_window = lax.dynamic_slice_in_dim(padded_values, offset_base, front_padding + TOK_DEV, 0)
        key_header = jnp.concatenate([lax.dynamic_slice_in_dim(keys_rank_three, target_start[index], HDR, 0) for index in range(block_count)], axis=0)
        value_header = jnp.concatenate([lax.dynamic_slice_in_dim(values_rank_three, target_start[index], HDR, 0) for index in range(block_count)], axis=0)
        key_all = jnp.concatenate([key_window, key_header], axis=0).astype(jnp.float32)
        value_all = jnp.concatenate([value_window, value_header], axis=0).astype(jnp.float32)
        visible = visibility(places, file_of, file_begin, key_places, source_file, usable, target_len)
        query_here = lax.dynamic_slice_in_dim(query_rank_four, offset_base, TOK_DEV, 0).astype(jnp.float32)
        grad_here = lax.dynamic_slice_in_dim(gradient_rank_four, offset_base, TOK_DEV, 0).astype(jnp.float32)
        scores = jnp.einsum('tagd,kad->agtk', query_here, key_all) * scaling
        scores = jnp.where(visible[None, None], scores, -jnp.inf)
        ceiling = lax.optimization_barrier(jnp.max(scores, axis=-1, keepdims=True))
        log_total = ceiling + jnp.log(lax.optimization_barrier(jnp.sum(jnp.exp(scores - ceiling), axis=-1, keepdims=True)))
        weights = jnp.exp(scores - log_total)
        grad_weights = jnp.einsum('tagd,kad->agtk', grad_here, value_all)
        centre = lax.optimization_barrier(jnp.sum(weights * grad_weights, axis=-1, keepdims=True))
        grad_scores = lax.optimization_barrier((weights * (grad_weights - centre)).astype(jnp.bfloat16)).astype(jnp.float32)
        weights_low = lax.optimization_barrier(weights.astype(jnp.bfloat16)).astype(jnp.float32)
        grad_query = jnp.einsum('agtk,kad->tagd', grad_scores, key_all) * scaling
        key_part = jnp.einsum('agtk,tagd->kad', grad_scores, query_here) * scaling
        value_part = jnp.einsum('agtk,tagd->kad', weights_low, grad_here)
        window_len = front_padding + TOK_DEV
        current = lax.dynamic_slice_in_dim(key_gradient_sum, offset_base, window_len, 0)
        key_gradient_sum = lax.dynamic_update_slice_in_dim(key_gradient_sum, current + key_part[:window_len], offset_base, 0)
        current = lax.dynamic_slice_in_dim(value_gradient_sum, offset_base, window_len, 0)
        value_gradient_sum = lax.dynamic_update_slice_in_dim(value_gradient_sum, current + value_part[:window_len], offset_base, 0)
        for index in range(block_count):
            at_row = (front_padding + target_start[index]).astype(jnp.int32)
            lower = window_len + index * HDR
            current = lax.dynamic_slice_in_dim(key_gradient_sum, at_row, HDR, 0)
            key_gradient_sum = lax.dynamic_update_slice_in_dim(key_gradient_sum, current + key_part[lower:lower + HDR], at_row, 0)
            current = lax.dynamic_slice_in_dim(value_gradient_sum, at_row, HDR, 0)
            value_gradient_sum = lax.dynamic_update_slice_in_dim(value_gradient_sum, current + value_part[lower:lower + HDR], at_row, 0)
        return ((key_gradient_sum, value_gradient_sum), grad_query.reshape(TOK_DEV, QUERY_HEADS * HEAD_WIDTH))
    empty_gradient = jnp.zeros((front_padding + PACKED_TOKENS, KEY_VALUE_HEADS, HEAD_WIDTH), jnp.float32)
    (key_gradient_sum, value_gradient_sum), grad_query = lax.scan(one_shard, (empty_gradient, empty_gradient), jnp.arange(shards, dtype=jnp.int32))
    grad_queries = grad_query.reshape(PACKED_TOKENS, QUERY_HEADS * HEAD_WIDTH)
    key_gradient = key_gradient_sum[front_padding:].reshape(PACKED_TOKENS, KEY_VALUE_HEADS * HEAD_WIDTH)
    value_gradient = value_gradient_sum[front_padding:].reshape(PACKED_TOKENS, KEY_VALUE_HEADS * HEAD_WIDTH)
    return (grad_queries, key_gradient, value_gradient)
```

```python
import functools
import math

import jax
import jax.numpy as jnp
from jax import lax
from jax.experimental import pallas as pl
from jax.experimental.pallas import tpu as pltpu
from jax.sharding import PartitionSpec as P

WIN = 1024
HDR = 64
NEG = -1e30
LOG2E = 1.4426950408889634
NT = (((1,), (1,)), ((), ()))
NN = (((1,), (0,)), ((), ()))
UNIT = 4
CHUNK = 192
VMEM = pltpu.VMEM


def attention_kernel(*refs, parts, files, per_file, heads, width):
    starts, imports, lens, where = refs[:4]
    table = refs[4]
    q_parts = refs[5 : 5 + parts]
    g_parts = refs[5 + parts : 5 + 2 * parts]
    outs = refs[5 + 2 * parts : 5 + 3 * parts]
    dkv_ref, kcat, vcat, kt, qaug, gall, sbuf, gwbuf, dcat, dqbuf, acc = refs[5 + 3 * parts :]
    t = pl.program_id(0)
    sub = lax.rem(where[1] - t + parts, parts)
    base = (where[0] * parts + sub) * HDR
    scaling = 1.0 / math.sqrt(width)
    full = WIN // HDR - 1
    lanes = UNIT * HDR
    total = kcat.shape[0]

    def count(i, best):
        return best + (starts[i] <= base).astype(jnp.int32)

    mine = lax.fori_loop(0, files, count, 0) - 1
    begin = starts[mine]

    rows, limits = [base, jnp.maximum(base - WIN, 0)], [None, base - WIN >= begin]
    for m in range(per_file):
        target = imports[mine * per_file + m]
        safe = jnp.maximum(target, 0)
        rows.append(starts[safe])
        limits.append(jnp.where(target >= 0, lens[safe], 0))
    for d in range(1, full + 1):
        rows.append(jnp.maximum(base - d * HDR, 0))
        limits.append(jnp.where(base - d * HDR >= begin, HDR, 0))

    kk = lax.broadcasted_iota(jnp.int32, (HDR, width), 0)
    ff = lax.broadcasted_iota(jnp.int32, (HDR, width), 1)

    @pl.when(t == 0)
    def _():
        acc[...] = jnp.zeros_like(acc)
        onehot = (kk == ff).astype(jnp.bfloat16)
        for h in range(heads):
            qaug[h * HDR : (h + 1) * HDR, width:] = onehot

    for p in range(parts):

        @pl.when(t == p)
        def _():
            for h in range(heads):
                at = slice(h * HDR, (h + 1) * HDR)
                qaug[at, :width] = q_parts[p][:, h * width : (h + 1) * width]
                gall[at, :] = g_parts[p][:, h * width : (h + 1) * width]

    for b, row in enumerate(rows):
        src = pl.ds(pl.multiple_of(row, HDR), HDR)
        dst = slice(b * HDR, (b + 1) * HDR)
        kcat[dst, :width] = table[src, :width]
        vcat[dst, :] = table[src, width:]
        if b == 0:
            hidden = kk > ff
        elif b == 1:
            hidden = kk <= jnp.where(limits[b], ff, HDR)
        else:
            hidden = kk >= limits[b]
        kcat[dst, width:] = jnp.where(hidden, NEG, 0.0).astype(jnp.bfloat16)

    chunks = total // CHUNK
    for j in range(chunks):
        kt[j] = kcat[j * CHUNK : (j + 1) * CHUNK, :width].T

    for u in range(heads // UNIT):
        lane = slice(u * lanes, (u + 1) * lanes)
        qa = qaug[lane, :]
        qu = qaug[lane, :width]
        gu = gall[lane, :]
        peak = jnp.full((8, lanes), -jnp.inf, jnp.float32)
        for j in range(chunks):
            at = slice(j * CHUNK, (j + 1) * CHUNK)
            s = lax.dot_general(kcat[at, :], qa, NT, preferred_element_type=jnp.float32)
            sbuf[u % 2, at, :] = s
            peak = jnp.maximum(peak, jnp.max(s.reshape(CHUNK // 8, 8, lanes), axis=0))
        peak = jnp.max(peak, axis=0, keepdims=True)
        norm = jnp.zeros((8, lanes), jnp.float32)
        centre = jnp.zeros((8, lanes), jnp.float32)
        for j in range(chunks):
            at = slice(j * CHUNK, (j + 1) * CHUNK)
            e = jnp.exp2((sbuf[u % 2, at, :] - peak) * (scaling * LOG2E))
            gw = lax.dot_general(vcat[at, :], gu, NT, preferred_element_type=jnp.float32)
            sbuf[u % 2, at, :] = e
            gwbuf[u % 2, at, :] = gw
            norm = norm + jnp.sum(e.reshape(CHUNK // 8, 8, lanes), axis=0)
            centre = centre + jnp.sum((e * gw).reshape(CHUNK // 8, 8, lanes), axis=0)
        inv = 1.0 / jnp.sum(norm, axis=0, keepdims=True)
        centre = jnp.sum(centre, axis=0, keepdims=True) * inv
        dqt = jnp.zeros((width, lanes), jnp.float32)
        for j in range(chunks):
            at = slice(j * CHUNK, (j + 1) * CHUNK)
            w = sbuf[u % 2, at, :] * inv
            ds = (w * (gwbuf[u % 2, at, :] - centre)).astype(jnp.bfloat16)
            w = w.astype(jnp.bfloat16)
            dk = lax.dot_general(ds, qu, NN, preferred_element_type=jnp.float32)
            dv = lax.dot_general(w, gu, NN, preferred_element_type=jnp.float32)
            dqt = dqt + lax.dot_general(kt[j], ds, NN, preferred_element_type=jnp.float32)
            if u == 0:
                dcat[at, :width] = dk
                dcat[at, width:] = dv
            else:
                dcat[at, :width] += dk
                dcat[at, width:] += dv
        dq = (dqt * scaling).T.astype(jnp.bfloat16)
        for i in range(UNIT):
            h = u * UNIT + i
            dqbuf[:, h * width : (h + 1) * width] = dq[i * HDR : (i + 1) * HDR, :]

    for p in range(parts):

        @pl.when(t == p)
        def _():
            outs[p][...] = dqbuf[...]

    for b, row in enumerate(rows):
        dst = pl.ds(pl.multiple_of(row, HDR), HDR)
        acc[dst, :] += dcat[b * HDR : (b + 1) * HDR, :]

    @pl.when(t == parts - 1)
    def _():
        dkv_ref[:, :width] = (acc[:, :width] * scaling).astype(dkv_ref.dtype)
        dkv_ref[:, width:] = acc[:, width:].astype(dkv_ref.dtype)


def attention(where, starts, imports, lens, table, q_parts, g_parts):
    parts = len(q_parts)
    rows, columns = q_parts[0].shape
    width = table.shape[1] // 2
    heads = columns // width
    files, per_file = imports.shape
    total = (WIN // HDR + 1 + per_file) * HDR
    lanes = UNIT * HDR
    whole = pl.BlockSpec(memory_space=VMEM)
    bf = jnp.bfloat16
    outs = pl.pallas_call(
        functools.partial(
            attention_kernel, parts=parts, files=files, per_file=per_file, heads=heads, width=width
        ),
        grid_spec=pltpu.PrefetchScalarGridSpec(
            num_scalar_prefetch=4,
            grid=(parts,),
            in_specs=[whole] * (1 + 2 * parts),
            out_specs=[whole] * (parts + 1),
            scratch_shapes=[
                VMEM((total, 2 * width), bf),
                VMEM((total, width), bf),
                VMEM((total // CHUNK, width, CHUNK), bf),
                VMEM((heads * HDR, 2 * width), bf),
                VMEM((heads * HDR, width), bf),
                VMEM((2, total, lanes), jnp.float32),
                VMEM((2, total, lanes), jnp.float32),
                VMEM((total, 2 * width), jnp.float32),
                VMEM((rows, columns), bf),
                VMEM((table.shape[0], 2 * width), jnp.float32),
            ],
        ),
        out_shape=[jax.ShapeDtypeStruct((rows, columns), bf)] * parts
        + [jax.ShapeDtypeStruct(table.shape, bf)],
        compiler_params=pltpu.CompilerParams(vmem_limit_bytes=60 << 20),
        name="attention",
    )(starts, imports.reshape(-1), lens, where, table, *q_parts, *g_parts)
    return outs[:parts], outs[parts]


def finish_kernel(*refs, parts, width):
    where = refs[0]
    gq_parts = refs[1 : 1 + parts]
    dkv = refs[1 + parts]
    gq_ref, dk_ref, dv_ref = refs[2 + parts :]
    columns = gq_parts[0].shape[1]
    for p in range(parts):
        head = lax.rem(where[1] + p, parts)
        at = pl.ds(pl.multiple_of(head * columns, columns), columns)
        gq_ref[:, at] = gq_parts[p][...].astype(jnp.float32)
    for a in range(parts):
        total = jnp.sum(dkv[:, a].astype(jnp.float32), axis=0)
        dk_ref[:, a * width : (a + 1) * width] = total[:, :width]
        dv_ref[:, a * width : (a + 1) * width] = total[:, width:]


def finish(where, gq_parts, dkv):
    parts = len(gq_parts)
    rows, columns = gq_parts[0].shape
    width = dkv.shape[-1] // 2
    whole = pl.BlockSpec(memory_space=VMEM)
    return pl.pallas_call(
        functools.partial(finish_kernel, parts=parts, width=width),
        grid_spec=pltpu.PrefetchScalarGridSpec(
            num_scalar_prefetch=1,
            grid=(),
            in_specs=[whole] * (parts + 1),
            out_specs=[whole] * 3,
        ),
        out_shape=[
            jax.ShapeDtypeStruct((rows, parts * columns), jnp.float32),
            jax.ShapeDtypeStruct((rows, parts * width), jnp.float32),
            jax.ShapeDtypeStruct((rows, parts * width), jnp.float32),
        ],
        compiler_params=pltpu.CompilerParams(vmem_limit_bytes=60 << 20),
        name="finish",
    )(where, *gq_parts, dkv)


def per_device(
    queries, key_head_columns, value_head_columns, output_gradient, file_starts, file_imports, header_lens
):
    blocks, parts = lax.axis_size("ctx"), lax.axis_size("head")
    rows = queries.shape[0]
    width = key_head_columns.shape[1] // parts
    columns = queries.shape[1] // parts
    everyone = ("ctx", "head")
    place, seat = lax.axis_index("ctx"), lax.axis_index("head")
    where = jnp.stack([place, seat]).astype(jnp.int32)

    def by_head(value):
        return value.reshape(rows, parts, width).transpose(1, 0, 2)

    pair = jnp.concatenate([by_head(key_head_columns), by_head(value_head_columns)], axis=2)
    sent = jnp.broadcast_to(pair[None], (blocks,) + pair.shape).reshape(blocks * parts, rows, 2 * width)
    table = lax.all_to_all(sent, everyone, split_axis=0, concat_axis=0, tiled=True)
    table = table.reshape(blocks * parts * rows, 2 * width)

    def exchange(value):
        out = []
        for step in range(parts):
            piece = lax.dynamic_slice_in_dim(value, lax.rem(seat + step, parts) * columns, columns, 1)
            if step:
                piece = lax.ppermute(piece, "head", [(s, (s + step) % parts) for s in range(parts)])
            out.append(piece)
        return out

    q_parts, g_parts = exchange(queries), exchange(output_gradient)
    gq_parts, dkv = attention(where, file_starts, file_imports, header_lens, table, q_parts, g_parts)
    back = lax.all_to_all(
        dkv.reshape(blocks * parts, rows, 2 * width), everyone, split_axis=0, concat_axis=0, tiled=True
    )
    home = [
        lax.ppermute(piece, "head", [((s + step) % parts, s) for s in range(parts)]) if step else piece
        for step, piece in enumerate(gq_parts)
    ]
    return tuple(finish(where, home, back.reshape(blocks, parts, rows, 2 * width)))


def solution(mesh):
    split = P(("ctx", "head"), None)
    return jax.shard_map(
        per_device,
        mesh=mesh,
        in_specs=(split, split, split, split, P(), P(), P()),
        out_specs=(split, split, split),
        check_vma=False,
    )
```

```python
import functools
import math

import jax
import jax.numpy as jnp
from jax import lax
from jax.experimental import pallas as pl
from jax.experimental.pallas import tpu as pltpu
from jax.sharding import PartitionSpec as P


WIN = 1024
HDR = 64
NEG = -1e30
LOG2E = 1.4426950408889634
NT = (((1,), (1,)), ((), ()))
NN = (((1,), (0,)), ((), ()))
UNIT = 4
CHUNK = 192
EARLY = ((0, 2), (2, 4))
VMEM = pltpu.VMEM


def attention_kernel(*refs, parts, files, per_file, heads, width, first, last):
    starts, imports, lens, bases, where = refs[:5]
    tables = refs[5:7]
    q_parts = refs[7 : 7 + parts]
    g_parts = refs[7 + parts : 7 + 2 * parts]
    refs = refs[7 + 2 * parts :]
    if not first:
        carried, refs = refs[0], refs[1:]
    outs, refs = refs[:parts], refs[parts:]
    if last:
        (kept, given), refs = refs[:2], refs[2:]
    else:
        carry, refs = refs[0], refs[1:]
    table, kcat, vcat, kt, qaug, gall, sbuf, gwbuf, dcat, dqbuf, acc, sems = refs
    t = pl.program_id(0)
    core = where[0]
    base = bases[t]
    scaling = 1.0 / math.sqrt(width)
    full = WIN // HDR - 1
    lanes = UNIT * HDR
    total = kcat.shape[0]
    chips = tables[0].shape[0]

    def fetch(index):
        which = core if index == 0 else 1 - core
        return pltpu.make_async_copy(tables[index], table.at[:, which], sems.at[index])

    @pl.when(t == 0)
    def _():
        for index in range(2):
            fetch(index).start()
        if not first:
            pltpu.make_async_copy(carried, acc, sems.at[2]).start()

    def count(i, best):
        return best + (starts[i] <= base).astype(jnp.int32)

    mine = lax.fori_loop(0, files, count, 0) - 1
    begin = starts[mine]

    rows, limits = [base, jnp.maximum(base - WIN, 0)], [None, base - WIN >= begin]
    for m in range(per_file):
        target = imports[mine * per_file + m]
        safe = jnp.maximum(target, 0)
        rows.append(starts[safe])
        limits.append(jnp.where(target >= 0, lens[safe], 0))
    for d in range(1, full + 1):
        rows.append(jnp.maximum(base - d * HDR, 0))
        limits.append(jnp.where(base - d * HDR >= begin, HDR, 0))
    rows = [lax.div(row, HDR) for row in rows]

    kk = lax.broadcasted_iota(jnp.int32, (HDR, width), 0)
    ff = lax.broadcasted_iota(jnp.int32, (HDR, width), 1)

    @pl.when(t == 0)
    def _():
        if first:
            acc[...] = jnp.zeros_like(acc)
        onehot = (kk == ff).astype(jnp.bfloat16)
        for h in range(heads):
            qaug[h * HDR : (h + 1) * HDR, width:] = onehot

    for p in range(parts):

        @pl.when(t == p)
        def _():
            for h in range(heads):
                at = slice(h * HDR, (h + 1) * HDR)
                qaug[at, :width] = q_parts[p][:, h * width : (h + 1) * width]
                gall[at, :] = g_parts[p][:, h * width : (h + 1) * width]

    @pl.when(t == 0)
    def _():
        for index in range(2):
            fetch(index).wait()

    for b, row in enumerate(rows):
        dst = slice(b * HDR, (b + 1) * HDR)
        block = table[lax.div(row, 2), lax.rem(row, 2)]
        kcat[dst, :width] = block[:, :width]
        vcat[dst, :] = block[:, width:]
        if b == 0:
            hidden = kk > ff
        elif b == 1:
            hidden = kk <= jnp.where(limits[b], ff, HDR)
        else:
            hidden = kk >= limits[b]
        kcat[dst, width:] = jnp.where(hidden, NEG, 0.0).astype(jnp.bfloat16)

    chunks = total // CHUNK
    for j in range(chunks):
        kt[j] = kcat[j * CHUNK : (j + 1) * CHUNK, :width].T

    for u in range(heads // UNIT):
        lane = slice(u * lanes, (u + 1) * lanes)
        qa = qaug[lane, :]
        qu = qaug[lane, :width]
        gu = gall[lane, :]
        peak = jnp.full((8, lanes), -jnp.inf, jnp.float32)
        for j in range(chunks):
            at = slice(j * CHUNK, (j + 1) * CHUNK)
            s = lax.dot_general(kcat[at, :], qa, NT, preferred_element_type=jnp.float32)
            sbuf[u % 2, at, :] = s
            peak = jnp.maximum(peak, jnp.max(s.reshape(CHUNK // 8, 8, lanes), axis=0))
        peak = jnp.max(peak, axis=0, keepdims=True)
        norm = jnp.zeros((8, lanes), jnp.float32)
        centre = jnp.zeros((8, lanes), jnp.float32)
        for j in range(chunks):
            at = slice(j * CHUNK, (j + 1) * CHUNK)
            e = jnp.exp2((sbuf[u % 2, at, :] - peak) * (scaling * LOG2E))
            gw = lax.dot_general(vcat[at, :], gu, NT, preferred_element_type=jnp.float32)
            sbuf[u % 2, at, :] = e
            gwbuf[u % 2, at, :] = gw
            norm = norm + jnp.sum(e.reshape(CHUNK // 8, 8, lanes), axis=0)
            centre = centre + jnp.sum((e * gw).reshape(CHUNK // 8, 8, lanes), axis=0)
        inv = 1.0 / jnp.sum(norm, axis=0, keepdims=True)
        centre = jnp.sum(centre, axis=0, keepdims=True) * inv
        dqt = jnp.zeros((width, lanes), jnp.float32)
        for j in range(chunks):
            at = slice(j * CHUNK, (j + 1) * CHUNK)
            w = sbuf[u % 2, at, :] * inv
            ds = (w * (gwbuf[u % 2, at, :] - centre)).astype(jnp.bfloat16)
            w = w.astype(jnp.bfloat16)
            dk = lax.dot_general(ds, qu, NN, preferred_element_type=jnp.float32)
            dv = lax.dot_general(w, gu, NN, preferred_element_type=jnp.float32)
            dqt = dqt + lax.dot_general(kt[j], ds, NN, preferred_element_type=jnp.float32)
            if u == 0:
                dcat[at, :width] = dk
                dcat[at, width:] = dv
            else:
                dcat[at, :width] += dk
                dcat[at, width:] += dv
        dq = (dqt * scaling).T.astype(jnp.bfloat16)
        for i in range(UNIT):
            h = u * UNIT + i
            dqbuf[:, h * width : (h + 1) * width] = dq[i * HDR : (i + 1) * HDR, :]

    for p in range(parts):

        @pl.when(t == p)
        def _():
            outs[p][...] = dqbuf[...]

    if not first:

        @pl.when(t == 0)
        def _():
            pltpu.make_async_copy(carried, acc, sems.at[2]).wait()

    for b, row in enumerate(rows):
        acc[row] += dcat[b * HDR : (b + 1) * HDR, :]

    @pl.when(t == parts - 1)
    def _():
        if last:
            for i in range(chips):
                for index, ref in enumerate((kept, given)):
                    block = acc[2 * i + (core if index == 0 else 1 - core)]
                    ref[i, :, :width] = (block[:, :width] * scaling).astype(ref.dtype)
                    ref[i, :, width:] = block[:, width:].astype(ref.dtype)
        else:
            pltpu.sync_copy(acc, carry)


def attention(core, bases, starts, imports, lens, tables, q_parts, g_parts, carried, last):
    parts = len(q_parts)
    rows, columns = q_parts[0].shape
    chips, block, pair = tables[0].shape
    width = pair // 2
    heads = columns // width
    files, per_file = imports.shape
    total = (WIN // HDR + 1 + per_file) * HDR
    lanes = UNIT * HDR
    whole = pl.BlockSpec(memory_space=VMEM)
    anywhere = pl.BlockSpec(memory_space=pl.ANY)
    bf = jnp.bfloat16
    first = carried is None
    all_rows = 2 * chips * block
    sums = (2 * chips, block, pair)
    if last:
        extra_specs = [whole, whole]
        extra = [jax.ShapeDtypeStruct(tables[0].shape, jnp.float32), jax.ShapeDtypeStruct(tables[0].shape, bf)]
    else:
        extra_specs = [anywhere]
        extra = [jax.ShapeDtypeStruct(sums, jnp.float32)]
    outs = pl.pallas_call(
        functools.partial(
            attention_kernel,
            parts=parts,
            files=files,
            per_file=per_file,
            heads=heads,
            width=width,
            first=first,
            last=last,
        ),
        grid_spec=pltpu.PrefetchScalarGridSpec(
            num_scalar_prefetch=5,
            grid=(parts,),
            in_specs=[anywhere] * 2 + [whole] * (2 * parts) + [anywhere] * (not first),
            out_specs=[whole] * parts + extra_specs,
            scratch_shapes=[
                VMEM((chips, 2, block, pair), bf),
                VMEM((total, pair), bf),
                VMEM((total, width), bf),
                VMEM((total // CHUNK, width, CHUNK), bf),
                VMEM((heads * HDR, pair), bf),
                VMEM((heads * HDR, width), bf),
                VMEM((2, total, lanes), jnp.float32),
                VMEM((2, total, lanes), jnp.float32),
                VMEM((total, pair), jnp.float32),
                VMEM((rows, columns), bf),
                VMEM(sums, jnp.float32),
                pltpu.SemaphoreType.DMA((3,)),
            ],
        ),
        out_shape=[jax.ShapeDtypeStruct((rows, columns), bf)] * parts + extra,
        compiler_params=pltpu.CompilerParams(vmem_limit_bytes=(20 << 20) + all_rows * pair * 9),
        name="attention",
    )(starts, imports.reshape(-1), lens, bases, core, *tables, *q_parts, *g_parts, *([] if first else [carried]))
    return outs[:parts], outs[parts:]


def finish_kernel(*refs, parts, width):
    where = refs[0]
    gq_parts = refs[1 : 1 + parts]
    dkv = refs[1 + parts]
    gq_ref, dk_ref, dv_ref = refs[2 + parts :]
    columns = gq_parts[0].shape[1]
    for p in range(parts):
        head = where[0] ^ p
        at = pl.ds(pl.multiple_of(head * columns, columns), columns)
        gq_ref[:, at] = gq_parts[p][...].astype(jnp.float32)
    for a in range(parts):
        total = jnp.sum(dkv[:, a].astype(jnp.float32), axis=0)
        dk_ref[:, a * width : (a + 1) * width] = total[:, :width]
        dv_ref[:, a * width : (a + 1) * width] = total[:, width:]


def finish(where, gq_parts, dkv):
    parts = len(gq_parts)
    rows, columns = gq_parts[0].shape
    width = dkv.shape[-1] // 2
    whole = pl.BlockSpec(memory_space=VMEM)
    return pl.pallas_call(
        functools.partial(finish_kernel, parts=parts, width=width),
        grid_spec=pltpu.PrefetchScalarGridSpec(
            num_scalar_prefetch=1,
            grid=(),
            in_specs=[whole] * (parts + 1),
            out_specs=[whole] * 3,
        ),
        out_shape=[
            jax.ShapeDtypeStruct((rows, parts * columns), jnp.float32),
            jax.ShapeDtypeStruct((rows, parts * width), jnp.float32),
            jax.ShapeDtypeStruct((rows, parts * width), jnp.float32),
        ],
        compiler_params=pltpu.CompilerParams(vmem_limit_bytes=60 << 20),
        name="finish",
    )(where, *gq_parts, dkv)


def per_device(
    queries, key_head_columns, value_head_columns, output_gradient, file_starts, file_imports, header_lens
):
    blocks, seats = lax.axis_size("ctx"), lax.axis_size("head")
    rows = queries.shape[0]
    parts = seats
    width = key_head_columns.shape[1] // parts
    columns = queries.shape[1] // parts
    everyone = ("ctx", "head")
    place, seat = lax.axis_index("ctx"), lax.axis_index("head")
    core = lax.rem(seat, 2)
    group = lax.rem(place, 2) * 2 + lax.div(seat, 2)
    chips = blocks * seats // 2

    def device(block, where, which):
        return block * seats + where * 2 + which

    def partners(step):
        pairs = []
        for block in range(blocks):
            for where in range(2):
                for which in range(2):
                    pairs.append(
                        (device(block, where, which), device(block ^ (step >> 1), where ^ (step & 1), which))
                    )
        return pairs

    siblings = [(s, s ^ 1) for s in range(seats)]
    same_core = [[device(b, w, which) for b in range(blocks) for w in range(2)] for which in range(2)]

    def spread(value):
        return lax.all_to_all(
            value, everyone, split_axis=0, concat_axis=0, tiled=True, axis_index_groups=same_core
        )

    def swap(value):
        return lax.ppermute(value, "head", siblings)

    def pass_on(value, step):
        if not step:
            return value
        return lax.ppermute(value, everyone, partners(step))

    def by_head(value):
        return value.reshape(rows, parts, width).transpose(1, 0, 2)

    pair = jnp.concatenate([by_head(key_head_columns), by_head(value_head_columns)], axis=2)
    sent = jnp.broadcast_to(pair[None], (chips // parts,) + pair.shape).reshape(chips, rows, 2 * width)
    mine = spread(sent)
    theirs = swap(mine)

    def exchange(value, step):
        piece = lax.dynamic_slice_in_dim(value, (group ^ step) * columns, columns, 1)
        return pass_on(piece, step)

    q_parts = [exchange(queries, step) for step in range(parts)]
    g_parts = [exchange(output_gradient, step) for step in range(parts)]
    bases = jnp.stack(
        [
            ((place ^ (step >> 1)) * seats + (seat ^ (2 * (step & 1)))) * rows
            for step in range(parts)
        ]
    ).astype(jnp.int32)
    lone = core.reshape(1).astype(jnp.int32)
    scalars = (file_starts, file_imports, header_lens, (mine, theirs))
    gq_parts, carried = [], None
    for low, high in EARLY:
        done, carried = attention(
            lone,
            bases[low:high],
            *scalars,
            q_parts[low:high],
            g_parts[low:high],
            carried,
            high == parts,
        )
        carried = carried[0] if high < parts else carried
        gq_parts += [pass_on(piece, step) for step, piece in enumerate(done, low)]
    kept, given = carried
    summed = (kept + swap(given).astype(jnp.float32)).astype(jnp.bfloat16)
    back = spread(summed).reshape(chips // parts, parts, rows, 2 * width)
    return tuple(finish(group.reshape(1).astype(jnp.int32), gq_parts, back))


def solution(mesh):
    split = P(("ctx", "head"), None)
    return jax.shard_map(
        per_device,
        mesh=mesh,
        in_specs=(split, split, split, split, P(), P(), P()),
        out_specs=(split, split, split),
        check_vma=False,
    )
```
